32 devices in a mesh: gx: 4 (over y, x), gy: 8 (over z, core).
Axes of the slice: x: 2, y: 2, z: 4, core: 2. Of those that a mesh axis runs over, the one named last changes fastest.
Arguments:
- links: float32 [4, 3, 3, 2, 8, 16, 6, 128], P(None, None, None, None, 'gx', 'gy'), may hold values from -1 to 1, as said below
- incoming: float32 [4, 3, 3, 2, 8, 16, 4, 128], P(None, None, None, None, 'gx', 'gy'), may hold values from -6 to 6
Outputs:
- force: float32 [4, 3, 3, 2, 8, 16, 4, 128], P(None, None, None, None, 'gx', 'gy')
The draws below stay inside these ranges and needn't reach their ends.
Inputs may be any that keep to these rules, and one draw needn't show every extreme that they name: `links`: each link is a special unitary 3 x 3 matrix.
All inputs are finite; a program needn't handle non-finite values.
Results may differ from the reference program's by a relative error of at most 0.0003.
Values sent between devices are 32-bit elements; how exact they have to be, the bound alone decides.
A program may use at most 128 MiB of HBM per device.

```python
from functools import partial
import jax
import jax.numpy as jnp
from jax import lax

Z = 128
TS = 4
NX = 8
NY = 16


phase_rows = [[0.0, 0.6, -0.6], [0.3, 0.0, -0.3], [0.6, 0.9, -1.5], [0.9, 0.3, -1.2]]


def special_unitary(matrix):
    row_one = matrix[..., 0, :]
    row_one = row_one / jnp.sqrt(jnp.sum(jnp.abs(row_one) ** 2, axis=-1, keepdims=True))
    row_two = matrix[..., 1, :]
    row_two = row_two - jnp.sum(jnp.conj(row_one) * row_two, axis=-1, keepdims=True) * row_one
    row_two = row_two / jnp.sqrt(jnp.sum(jnp.abs(row_two) ** 2, axis=-1, keepdims=True))
    row_three = jnp.conj(jnp.cross(row_one, row_two))
    return jnp.stack([row_one, row_two, row_three], axis=-2)


def matmul_three(former, latter):
    return jnp.einsum('...ij,...jk->...ik', former, latter, precision=lax.Precision.HIGHEST)


def draw_links(key, part):
    gauge_key, noise_key = jax.random.split(jax.random.fold_in(key, 17))
    real_key, imag_key = jax.random.split(gauge_key)
    noise_real_key, noise_imag_key = jax.random.split(noise_key)
    gauge_shape = (NX, NY, TS + 3, Z, 3, 3)
    noise_shape = (4, NX, NY, TS + 2, Z, 3, 3)
    identity = jnp.eye(3, dtype=jnp.float32)
    gauge_real = jax.random.normal(real_key, gauge_shape, jnp.float32)
    gauge_imag = jax.random.normal(imag_key, gauge_shape, jnp.float32)
    noise_real = jax.random.normal(noise_real_key, noise_shape, jnp.float32)
    noise_imag = jax.random.normal(noise_imag_key, noise_shape, jnp.float32)
    gauge = special_unitary(gauge_real + 1j * gauge_imag)
    noise = special_unitary(6.0 * identity + noise_real + 1j * noise_imag)
    coord_x = jnp.arange(NX, dtype=jnp.int32)[:, None, None, None]
    coord_y = jnp.arange(NY, dtype=jnp.int32)[None, :, None, None]
    coord_t = jnp.arange(TS + 2, dtype=jnp.int32)[None, None, :, None]
    coord_z = jnp.arange(Z, dtype=jnp.int32)[None, None, None, :]
    parity = (coord_x + coord_y + coord_t + coord_z) % 2
    sign = 1.0 - 2.0 * parity.astype(jnp.float32)
    table = jnp.array(phase_rows, dtype=jnp.float32)
    angle = table[:, None, None, None, None, :] * sign[None, :, :, :, :, None]
    backbone = jnp.exp(1j * angle)[..., :, None] * identity
    core = matmul_three(backbone, noise)
    here = gauge[:, :, :TS + 2]
    aheads = [jnp.roll(here, -1, axis=0), jnp.roll(here, -1, axis=1), jnp.roll(here, -1, axis=3), gauge[:, :, 1:TS + 3]]
    result = []
    for direction in range(4):
        ahead_dagger = jnp.conj(jnp.swapaxes(aheads[direction], -1, -2))
        result.append(matmul_three(matmul_three(here, core[direction]), ahead_dagger))
    unitary = jnp.stack(result, axis=0)
    stacked = jnp.stack([jnp.real(unitary), jnp.imag(unitary)], axis=-1).astype(jnp.float32)
    return jnp.transpose(stacked, (0, 5, 6, 7, 1, 2, 3, 4))


def shard_levels(rng, shape, cuts, least, largest):
    level, own = 1.0, jax.random.fold_in(rng, 6)
    for position, shards_of in cuts:
        steps = jnp.exp(jax.random.uniform(jax.random.fold_in(own, position), (shards_of,), jnp.float32, least / len(cuts), largest / len(cuts)))
        level = level * jnp.repeat(steps, shape[position] // shards_of).reshape([-1 if axis == position else 1 for axis in range(len(shape))])
    return level


def gaussian(rng, dims, scale, limit, cuts=(), kind=jnp.bfloat16):
    values = scale * jax.random.normal(rng, dims, jnp.float32)
    if cuts:
        values = values * shard_levels(rng, dims, cuts, -0.22, 0.18)
    return jnp.clip(values, -limit, limit).astype(kind)


def setup_inputs(seed: int = 0) -> dict:
    arg_keys = jax.random.split(jax.random.key(seed), 3)
    links = draw_links(jax.random.fold_in(arg_keys[2], 71), 0)
    incoming = gaussian(arg_keys[1], (4, 3, 3, 2, NX, NY, TS, Z), 1.0, 6.0, ((4, 4), (5, 8)), jnp.float32)
    return {"links": links, "incoming": incoming}


smear_weight = 0.2

def product(former, latter):
    former_real, former_imag = former
    latter_real, latter_imag = latter
    real_part = lax.optimization_barrier(jnp.sum(former_real[:, :, None] * latter_real[None] - former_imag[:, :, None] * latter_imag[None], axis=1))
    imag_part = lax.optimization_barrier(jnp.sum(former_real[:, :, None] * latter_imag[None] + former_imag[:, :, None] * latter_real[None], axis=1))
    return (real_part, imag_part)

def adjoint(matrix):
    return (jnp.swapaxes(matrix[0], 0, 1), -jnp.swapaxes(matrix[1], 0, 1))

def summed(former, latter):
    return (former[0] + latter[0], former[1] + latter[1])

def unit_step(which, sign):
    vector = [0, 0, 0, 0]
    vector[which] = sign
    return vector

def offset_list():
    result = [(0, 0, 0, 0)]
    for first in range(4):
        result.append(tuple(unit_step(first, 1)))
        result.append(tuple(unit_step(first, -1)))
        for second in range(4):
            if second != first:
                vector = unit_step(first, 1)
                vector[second] = -1
                result.append(tuple(vector))
    return result

def smeared_term(pieces, incoming, direction):

    def take(which, offset):
        block = pieces[str(tuple(offset))][which]
        return (block[:, :, 0], block[:, :, 1])
    anchor = [0, 0, 0, 0]
    ahead = unit_step(direction, 1)
    own = take(direction, anchor)
    staple = None
    for other in range(4):
        if other == direction:
            continue
        beside = unit_step(other, 1)
        behind = unit_step(other, -1)
        diagonal = [behind[k] + ahead[k] for k in range(4)]
        upper = product(product(take(other, anchor), take(direction, beside)), adjoint(take(other, ahead)))
        lower = product(product(adjoint(take(other, behind)), take(direction, behind)), take(other, diagonal))
        both = summed(upper, lower)
        staple = both if staple is None else summed(staple, both)
    staple = (smear_weight * staple[0], smear_weight * staple[1])
    omega = product(staple, adjoint(own))
    flipped = adjoint(omega)
    anti_real = 0.5 * (omega[0] - flipped[0])
    anti_imag = 0.5 * (omega[1] - flipped[1])
    identity = jnp.eye(3, dtype=jnp.float32)[:, :, None, None, None, None]
    trace_real = anti_real[0, 0] + anti_real[1, 1] + anti_real[2, 2]
    trace_imag = anti_imag[0, 0] + anti_imag[1, 1] + anti_imag[2, 2]
    anti = (anti_real - identity * trace_real / 3.0, anti_imag - identity * trace_imag / 3.0)
    result = (jnp.broadcast_to(identity, anti[0].shape), jnp.zeros_like(anti[1]))
    for order in range(6, 0, -1):
        stepped = product(anti, result)
        result = (identity + stepped[0] / order, stepped[1] / order)
    smeared = product(result, own)
    target = incoming[direction]
    return jnp.sum(target[:, :, 0] * smeared[0] + target[:, :, 1] * smeared[1])

def smear_loss(padded, incoming):
    region_x = padded.shape[4] - 2
    region_y = padded.shape[5] - 2
    slab = incoming.shape[6]
    depth = padded.shape[7]
    wrapped = jnp.concatenate([padded[..., depth - 1:], padded, padded[..., :1]], axis=7)
    pieces = {}
    for offset in offset_list():
        pieces[str(offset)] = wrapped[:, :, :, :, 1 + offset[0]:1 + offset[0] + region_x, 1 + offset[1]:1 + offset[1] + region_y, 1 + offset[3]:1 + offset[3] + slab, 1 + offset[2]:1 + offset[2] + depth]
    total = jnp.float32(0.0)
    for direction in range(4):
        total = total + jax.checkpoint(partial(smeared_term, direction=direction))(pieces, incoming)
    return total

def reference(links, incoming):
    slab = incoming.shape[6]

    def whole_loss(field):
        padded = jnp.pad(field, ((0, 0),) * 4 + ((1, 1), (1, 1)) + ((0, 0), (0, 0)), mode='wrap')
        return smear_loss(padded, incoming)
    grads = jax.grad(whole_loss)(links)
    return grads[:, :, :, :, :, :, 1:1 + slab]
```

```python
from functools import partial

import jax
import jax.numpy as jnp
from jax import lax
from jax.experimental import pallas as pl
from jax.experimental.pallas import tpu as pltpu
from jax.sharding import PartitionSpec as P

smear_weight = 0.2
MESH = pl.DeviceIdType.MESH
AXX, AXY, AXZ, AXT = 0, 1, 2, 3
SENT = 12
COMP = 18
ALG = 8
YSLOT = (1, 0, 2, 3)


def re(i, j):
    return (i * 3 + j) * 2


def conj(e):
    return (e[0], e[1], e[2], -e[3])


def dot(pairs, init=None, sign=1, parts="ri"):
    terms = {"r": [], "i": []}
    for a, b in pairs:
        for part, u, v, s in (
            ("r", 0, 0, a[2] * b[2]), ("r", 1, 1, -a[3] * b[3]),
            ("i", 0, 1, a[2] * b[3]), ("i", 1, 0, a[3] * b[2]),
        ):
            if part in parts and a[u] is not None and b[v] is not None:
                terms[part].append((sign * s, a[u], b[v]))
    out = []
    for k, part in enumerate("ri"):
        if part not in parts:
            out.append(None)
            continue
        todo = sorted(terms[part], key=lambda t: -t[0])
        total = None if init is None else init[k]
        for s, u, v in todo:
            w = u * v
            if total is None:
                total = w if s > 0 else -w
            else:
                total = total + w if s > 0 else total - w
        out.append(total)
    return tuple(out)


def elements(values):
    rows = [[(values[re(i, j)], values[re(i, j) + 1], 1, 1) for j in range(3)] for i in range(3)]
    return lambda i, j: rows[i][j]


def adjoint(mat):
    return lambda i, j: conj(mat(j, i))


def su3_product(a, b):
    rows = [[dot([(a(i, k), b(k, j)) for k in range(3)]) for j in range(3)] for i in range(2)]
    rows.append(third_row(rows))
    return [v for row in rows for e in row for v in e]


def third_row(rows):
    out = []
    for k in range(3):
        p, q = (k + 1) % 3, (k + 2) % 3
        a, b = [[(*e, 1, 1) for e in row] for row in rows]
        neg = (a[q][0], a[q][1], -1, -1)
        r, i = dot([(a[p], b[q]), (neg, b[p])], parts="r")[0], None
        i = a[q][0] * b[p][1] + a[q][1] * b[p][0] - a[p][0] * b[q][1] - a[p][1] * b[q][0]
        out.append((r, i))
    return out


def alg_elements(v):
    last = v[0] + v[1]
    diag = ((None, v[0], 1, 1), (None, v[1], 1, 1), (None, last, 1, -1))
    place = {(0, 1): 2, (0, 2): 4, (1, 2): 6}

    def get(i, j):
        if i == j:
            return diag[i]
        k = place[(min(i, j), max(i, j))]
        return (v[k], v[k + 1], 1 if i < j else -1, 1)
    return get


UPPER = ((0, 1), (0, 2), (1, 2))


def transport(g, x):
    half = [[(*dot([(g(i, k), x(k, j)) for k in range(3)]), 1, 1) for j in range(3)] for i in range(2)]
    out = [dot([(half[i][k], conj(g(i, k))) for k in range(3)], parts="i")[1] for i in range(2)]
    for i, j in UPPER:
        out += list(dot([(half[i][k], conj(g(j, k))) for k in range(3)]))
    return out


def kernel(
    sizes, links_hbm, inc_hbm, out,
    raw, inc, own, plus, prod, upper, low, lowy, tmin, tdia,
    sig, cst, lam, ahead, theta, thy,
    hxp, hyp, hly, bx0s, by0s, bx0, by0, ydn, yup,
    lxp, lyp, tyh, lydn, tyup,
    load_sem, send_sem, recv_sem,
):
    nx, ny = sizes
    wx, ts, wy, lanes = raw.shape[2], raw.shape[3] - 2, raw.shape[4], raw.shape[5]
    rows = wy * ts
    mx, my = lax.axis_index("gx"), lax.axis_index("gy")
    xu, xd = lax.rem(mx + 1, nx), lax.rem(mx + nx - 1, nx)
    yu, yd = lax.rem(my + 1, ny), lax.rem(my + ny - 1, ny)
    east, west, north, south = (xu, my), (xd, my), (mx, yu), (mx, yd)
    peers = (east, west, north, south)

    barrier = pltpu.get_barrier_semaphore()
    for peer in peers:
        pl.semaphore_signal(barrier, inc=1, device_id=peer, device_id_type=MESH)
    fetch = pltpu.make_async_copy(links_hbm, raw, load_sem.at[0])
    fetch.start()
    fetch_in = pltpu.make_async_copy(inc_hbm, inc, load_sem.at[1])
    fetch_in.start()

    row_id = lax.broadcasted_iota(jnp.int32, (rows, lanes), 0)
    y_id = lax.rem(row_id, wy)
    flat = raw.reshape(*raw.shape[:3], (ts + 2) * wy, lanes)

    def sub(v, shift):
        shift = shift % rows
        return v if shift == 0 else pltpu.roll(v, shift, 0)

    def lane(v, shift):
        return pltpu.roll(v, shift % lanes, 1)

    def pack_down(parts):
        v = parts[0]
        for x in range(1, wx):
            v = jnp.where(y_id == x, sub(parts[x], x), v)
        return v

    def pack_up(parts):
        v = sub(parts[0], 1 - wy)
        for x in range(1, wx):
            v = jnp.where(y_id == x, sub(parts[x], x + 1 - wy), v)
        return v

    def y_ahead(v, halo, x):
        return jnp.where(y_id == wy - 1, sub(halo, wy - 1 - x), sub(v, -1))

    def y_from_behind(v, halo, x):
        return jnp.where(y_id == 0, sub(halo, -x), sub(v, 1))

    def t_ahead(v):
        return jnp.where(row_id >= rows - wy, 0.0, sub(v, -wy))

    def t_behind(v):
        return jnp.where(row_id < wy, 0.0, sub(v, wy))

    def loop(n, body):
        def step(k, _):
            body(k)
            return 0
        lax.fori_loop(0, n, step, 0)

    count = [0]

    def send(src, dst, peer):
        k = count[0]
        count[0] += 1
        copy = pltpu.make_async_remote_copy(
            src_ref=src, dst_ref=dst, send_sem=send_sem.at[k],
            recv_sem=recv_sem.at[k], device_id=peer, device_id_type=MESH)
        copy.start()
        return copy

    s = pl.ds(0, SENT)
    fetch.wait()

    def compact(c):
        for d in range(4):
            for x in range(wx):
                own[d, c, x] = flat[d, c, x, wy:wy + rows, :]
    loop(COMP, compact)

    def edges(c):
        for d in (AXX, AXZ, AXT):
            ydn[YSLOT[d], c] = pack_down([own[d, c, x] for x in range(wx)])
        bx0s[c] = flat[AXT, c, 0, 0:wy, :]
        for x in range(wx):
            by0s[c, x:x + 1, :] = flat[AXT, c, x, 0:1, :]
    loop(SENT, edges)

    pl.semaphore_wait(barrier, len(peers))
    down_y = [send(ydn.at[1:4], hyp.at[1:4, s], south), send(by0s, by0.at[s], south)]
    down_x = [send(own.at[1:4, s, 0], hxp.at[1:4, s], west), send(bx0s, bx0.at[s], west)]

    def shifts(c):
        for d in range(4):
            for x in range(wx):
                tmin[d, c, x] = flat[d, c, x, 0:rows, :]
                if d != AXT:
                    plus[d, AXT, c, x] = flat[d, c, x, 2 * wy:2 * wy + rows, :]
                if d != AXZ:
                    plus[d, AXZ, c, x] = lane(own[d, c, x], -1)
        for x in range(wx):
            tdia[AXZ, c, x] = lane(tmin[AXT, c, x], -1)
    loop(COMP, shifts)

    def matrix(ref, *index):
        return elements([ref[(*index[:-1], c, index[-1])] for c in range(COMP)])

    def product(m, n, x):
        return su3_product(matrix(own, m, x), matrix(plus, n, m, x))

    def path(m, n):
        def body(x):
            p = product(m, n, x)
            for c, v in enumerate(p):
                prod[m, n, c, x] = v
            if n == AXT:
                p = su3_product(matrix(tmin, m, x), matrix(tdia, m, x))
                d = matrix(tmin, AXT, x)
            else:
                d = matrix(own, n, x)
            back = su3_product(adjoint(d), elements(p))
            for c, v in enumerate(back):
                if n == AXX:
                    low[m, n, c, x + 1] = v
                elif n == AXY:
                    lowy[m, c, x] = v
                elif n == AXZ:
                    low[m, n, c, x] = lane(v, 1)
                else:
                    low[m, n, c, x] = v
        loop(wx, body)

    def above(m, n):
        def body(x):
            r = su3_product(matrix(prod, n, m, x), adjoint(matrix(plus, n, m, x)))
            for c, v in enumerate(r):
                upper[m, n, c, x] = v
        loop(wx, body)

    def send_low_x(m):
        return send(low.at[m, AXX, s, wx], low.at[m, AXX, s, 0], east)

    def send_low_y(m):
        slot = YSLOT[m]

        def body(c):
            yup[slot, c] = pack_up([lowy[m, c, x] for x in range(wx)])
        loop(SENT, body)
        return send(yup.at[slot], hly.at[slot, s], north)

    def fix(ref, *index):
        rows_ = [[(ref[(*index, re(i, j))], ref[(*index, re(i, j) + 1)]) for j in range(3)] for i in range(2)]
        for k, e in enumerate(third_row(rows_)):
            ref[(*index, re(2, k))] = e[0]
            ref[(*index, re(2, k) + 1)] = e[1]

    up_x, up_y = [], []
    for m in (AXZ, AXT):
        path(m, AXX)
        up_x.append(send_low_x(m))
    for m in (AXZ, AXT):
        path(m, AXY)
        up_y.append(send_low_y(m))
    path(AXZ, AXT)
    path(AXT, AXZ)
    above(AXZ, AXT)
    above(AXT, AXZ)

    def convert(c):
        for d in range(4):
            for x in range(wx):
                for y in range(wy):
                    sig[d, c, x, pl.ds(y, ts, stride=wy), :] = inc[d, c, x, y]
    fetch_in.wait()
    loop(COMP, convert)

    for copy in down_y:
        copy.wait()
    loop(3, lambda d: fix(hyp, d + 1))
    fix(by0)

    def build_y(c):
        for d in (AXX, AXZ, AXT):
            for x in range(wx):
                plus[d, AXY, c, x] = y_ahead(own[d, c, x], hyp[YSLOT[d], c], x)
        for x in range(wx):
            edge = jnp.broadcast_to(by0[c, x:x + 1, :], (rows, lanes))
            v = jnp.where(row_id < wy, edge, sub(plus[AXT, AXY, c, x], wy))
            tdia[AXY, c, x] = jnp.where(row_id < wy - 1, sub(tmin[AXT, c, x], -1), v)
    loop(COMP, build_y)
    path(AXY, AXX)
    up_x.append(send_low_x(AXY))
    path(AXY, AXZ)
    path(AXY, AXT)
    for m in (AXZ, AXT):
        above(AXY, m)
        above(m, AXY)

    for copy in down_x:
        copy.wait()
    loop(3, lambda d: fix(hxp, d + 1))
    fix(bx0)

    def build_x(c):
        for d in (AXY, AXZ, AXT):
            for x in range(wx):
                plus[d, AXX, c, x] = own[d, c, x + 1] if x + 1 < wx else hxp[d, c]
        for x in range(wx - 1):
            tdia[AXX, c, x] = tmin[AXT, c, x + 1]
        edge = jnp.concatenate([bx0[c]] * ts, axis=0)
        tdia[AXX, c, wx - 1] = jnp.where(row_id < wy, edge, sub(hxp[AXT, c], wy))
    loop(COMP, build_x)
    path(AXX, AXY)
    up_y.append(send_low_y(AXX))
    path(AXX, AXZ)
    path(AXX, AXT)
    for m in (AXY, AXZ, AXT):
        above(AXX, m)
        above(m, AXX)

    def fix_low(m):
        first = [[(low[m, AXX, re(i, j), 0], low[m, AXX, re(i, j) + 1, 0]) for j in range(3)] for i in range(2)]
        for k, e in enumerate(third_row(first)):
            low[m, AXX, re(2, k), 0] = e[0]
            low[m, AXX, re(2, k) + 1, 0] = e[1]

    def finish_y(m):
        slot = YSLOT[m]
        fix(hly, slot)

        def body(c):
            for x in range(wx):
                low[m, AXY, c, x] = y_from_behind(lowy[m, c, x], hly[slot, c], x)
        loop(COMP, body)

    def algebra(m, x):
        u, target = matrix(own, m, x), matrix(sig, m, x)
        others = [n for n in range(4) if n != m]
        total = []
        for c in range(COMP):
            v = None
            for n in others:
                w = upper[m, n, c, x] + low[m, n, c, x]
                v = w if v is None else v + w
            total.append(smear_weight * v)
        staple = elements(total)

        def times_udag(left, i, j, parts="ri"):
            return dot([(left(i, k), conj(u(j, k))) for k in range(3)], parts=parts)

        diag = [times_udag(staple, i, i, "i")[1] for i in range(3)]
        third = (diag[0] + diag[1] + diag[2]) * (1.0 / 3.0)
        av = [diag[0] - third, diag[1] - third]
        for i, j in UPPER:
            p1, p2 = times_udag(staple, i, j), times_udag(staple, j, i)
            av += [0.5 * (p1[0] - p2[0]), 0.5 * (p1[1] + p2[1])]
        a = alg_elements(av)
        sq = {}
        for i in range(3):
            sq[(i, i)] = (dot([(a(i, k), a(k, i)) for k in range(3)], parts="r")[0], None, 1, 1)
        for i, j in UPPER:
            sq[(i, j)] = (*dot([(a(i, k), a(k, j)) for k in range(3)]), 1, 1)
            sq[(j, i)] = conj(sq[(i, j)])
        p = 0.5 * (sq[(0, 0)][0] + sq[(1, 1)][0] + sq[(2, 2)][0])
        every = [(i, j) for i in range(3) for j in range(3)]
        det = dot([(sq[(i, j)], a(j, i)) for i, j in every], parts="i")[1] * (1.0 / 3.0)
        f0 = (1.0 - det * det * (1.0 / 720), det * (1.0 / 6 + p * (1.0 / 120)))
        f1 = (1.0 + p * (1.0 / 6 + p * (1.0 / 120)), det * (1.0 / 24 + p * (1.0 / 360)), 1, 1)
        f2 = (0.5 + p * (1.0 / 24 + p * (1.0 / 720)), det * (1.0 / 120), 1, 1)
        e = {}
        for i, j in every:
            init = f0 if i == j else None
            e[(i, j)] = (*dot([(f1, a(i, j)), (f2, sq[(i, j)])], init=init), 1, 1)
        for i, j in every:
            v = dot([(conj(e[(k, i)]), target(k, j)) for k in range(3)])
            cst[m, re(i, j), x] = v[0]
            cst[m, re(i, j) + 1, x] = v[1]
        cot = {}
        for i, j in every:
            cot[(i, j)] = (*times_udag(target, i, j), 1, 1)
        t0 = (cot[(0, 0)][0] + cot[(1, 1)][0] + cot[(2, 2)][0],
              -(cot[(0, 0)][1] + cot[(1, 1)][1] + cot[(2, 2)][1]))
        t1 = dot([(conj(cot[ij]), a(*ij)) for ij in every])
        t2 = dot([(conj(cot[ij]), sq[ij]) for ij in every])
        p_bar = (-t0[1] * det * (1.0 / 120) + t1[0] * (1.0 / 6 + p * (1.0 / 60))
                 - t1[1] * det * (1.0 / 360) + t2[0] * (1.0 / 24 + p * (1.0 / 360)))
        d_bar = (-t0[0] * det * (1.0 / 360) - t0[1] * (1.0 / 6 + p * (1.0 / 120))
                 - t1[1] * (1.0 / 24 + p * (1.0 / 360)) - t2[1] * (1.0 / 120))
        g1, g2 = conj(f1), conj(f2)
        herm = {}
        for i in range(3):
            herm[(i, i)] = (dot([(g2, cot[(i, i)])], parts="r")[0], None, 1, 1)
        for i, j in UPPER:
            k1, k2 = dot([(g2, cot[(i, j)])]), dot([(g2, cot[(j, i)])])
            herm[(i, j)] = (0.5 * (k1[0] + k2[0]), 0.5 * (k1[1] - k2[1]), 1, 1)
            herm[(j, i)] = conj(herm[(i, j)])

        def both(i, j, parts="ri"):
            return dot([(a(i, k), herm[(k, j)]) for k in range(3)], parts=parts)

        diag = []
        for i in range(3):
            v = dot([(g1, cot[(i, i)])], parts="i")[1] - 2.0 * both(i, i, "i")[1]
            ai = a(i, i)
            w = p_bar * ai[1]
            v = v - w if ai[3] > 0 else v + w
            diag.append(v + d_bar * sq[(i, i)][0])
        third = (diag[0] + diag[1] + diag[2]) * (1.0 / 3.0)
        lv = [diag[0] - third, diag[1] - third]
        for i, j in UPPER:
            j1, j2 = dot([(g1, cot[(i, j)])]), dot([(g1, cot[(j, i)])])
            x1, x2 = both(i, j), both(j, i)
            aa, aq = a(i, j), sq[(i, j)]
            lv.append(0.5 * (j1[0] - j2[0]) - (x1[0] - x2[0]) - p_bar * aa[0] - d_bar * aq[1])
            lv.append(0.5 * (j1[1] + j2[1]) - (x1[1] + x2[1]) - p_bar * aa[1] + d_bar * aq[0])
        for k, v in enumerate(lv):
            lam[m, k, x] = smear_weight * v

    def send_lam(m):
        copies_x, copies_y = [], []
        if m != AXX:
            copies_x.append(send(lam.at[m, :, 0], lxp.at[m], west))
        if m != AXY:
            slot = YSLOT[m]
            for k in range(ALG):
                lydn[slot, k] = pack_down([lam[m, k, x] for x in range(wx)])
            copies_y.append(send(lydn.at[slot], lyp.at[slot], south))
        return copies_x, copies_y

    lam_x, lam_y = [], []
    for k, m in enumerate((AXZ, AXT, AXY, AXX)):
        if m != AXX:
            up_x[k].wait()
            fix_low(m)
        if m != AXY:
            up_y[min(k, 2)].wait()
            finish_y(m)
        loop(wx, partial(algebra, m))
        cx, cy = send_lam(m)
        lam_x += cx
        lam_y += cy

    def algebra_of(ref, *index):
        return [ref[(*index[:-1], k, index[-1])] for k in range(ALG)]

    def turn(n, m):
        def body(x):
            far = alg_elements(algebra_of(ahead, m, n, x))
            near_n, near_m = algebra_of(lam, n, x), algebra_of(lam, m, x)
            un = matrix(own, n, x)
            xs = [v + (b - c) for v, b, c in zip(transport(un, far), near_n, near_m)]
            xe = alg_elements(xs)
            for k, v in enumerate(transport(adjoint(matrix(own, m, x)), xe)):
                if m == AXX:
                    theta[n, m, k, x + 1] = v
                elif m == AXY:
                    thy[n, k, x] = v
                elif m == AXZ:
                    theta[n, m, k, x] = lane(v, 1)
                else:
                    theta[n, m, k, x] = t_behind(v)
            r = matrix(upper, m, n, x)
            for i in range(3):
                for j in range(3):
                    c = re(i, j)
                    v = dot([(xe(i, k), r(k, j)) for k in range(3)], init=(cst[m, c, x], cst[m, c + 1, x]))
                    cst[m, c, x] = v[0]
                    cst[m, c + 1, x] = v[1]
            r = matrix(upper, n, m, x)
            for i in range(3):
                for j in range(3):
                    c = re(i, j)
                    v = dot([(r(i, k), far(k, j)) for k in range(3)], init=(cst[n, c, x], cst[n, c + 1, x]), sign=-1)
                    cst[n, c, x] = v[0]
                    cst[n, c + 1, x] = v[1]
        loop(wx, body)

    def below(m, n):
        def body(x):
            xs = [b - c for b, c in zip(algebra_of(theta, m, n, x), algebra_of(lam, m, x))]
            xe, r = alg_elements(xs), matrix(low, m, n, x)
            for i in range(3):
                for j in range(3):
                    c = re(i, j)
                    v = dot([(xe(i, k), r(k, j)) for k in range(3)], init=(cst[m, c, x], cst[m, c + 1, x]))
                    cst[m, c, x] = v[0]
                    cst[m, c + 1, x] = v[1]
        loop(wx, body)

    def send_theta_x(n):
        return send(theta.at[n, AXX, :, wx], theta.at[n, AXX, :, 0], east)

    def send_theta_y(n):
        slot = YSLOT[n]
        for k in range(ALG):
            tyup[slot, k] = pack_up([thy[n, k, x] for x in range(wx)])
        return send(tyup.at[slot], tyh.at[slot], north)

    def look_zt(k):
        for m in range(4):
            for x in range(wx):
                if m != AXZ:
                    ahead[m, AXZ, k, x] = lane(lam[m, k, x], -1)
                if m != AXT:
                    ahead[m, AXT, k, x] = t_ahead(lam[m, k, x])
    loop(ALG, look_zt)
    th_x, th_y = [], []
    for n in (AXZ, AXT):
        turn(n, AXX)
        th_x.append(send_theta_x(n))
    for n in (AXZ, AXT):
        turn(n, AXY)
        th_y.append(send_theta_y(n))
    turn(AXZ, AXT)
    turn(AXT, AXZ)

    for copy in lam_y:
        copy.wait()

    def look_y(k):
        for m in (AXX, AXZ, AXT):
            for x in range(wx):
                ahead[m, AXY, k, x] = y_ahead(lam[m, k, x], lyp[YSLOT[m], k], x)
    loop(ALG, look_y)
    turn(AXY, AXX)
    th_x.append(send_theta_x(AXY))
    turn(AXY, AXZ)
    turn(AXY, AXT)

    for copy in lam_x:
        copy.wait()

    def look_x(k):
        for m in (AXY, AXZ, AXT):
            for x in range(wx):
                ahead[m, AXX, k, x] = lam[m, k, x + 1] if x + 1 < wx else lxp[m, k]
    loop(ALG, look_x)
    turn(AXX, AXY)
    th_y.append(send_theta_y(AXX))
    turn(AXX, AXZ)
    turn(AXX, AXT)

    for m in range(4):
        for n in (AXZ, AXT):
            if m != n:
                below(m, n)
    for k, m in enumerate((AXZ, AXT, AXY)):
        th_x[k].wait()
        below(m, AXX)
    for k, m in enumerate((AXZ, AXT, AXX)):
        th_y[k].wait()

        def meet(k, m=m):
            for x in range(wx):
                theta[m, AXY, k, x] = y_from_behind(thy[m, k, x], tyh[YSLOT[m], k], x)
        loop(ALG, meet)
        below(m, AXY)

    def deliver(c):
        for d in range(4):
            for x in range(wx):
                for y in range(wy):
                    out[d, c, x, y * ts:(y + 1) * ts, :] = cst[d, c, x, pl.ds(y, ts, stride=wy), :]
    loop(COMP, deliver)


def solution(mesh):
    sizes = (mesh.shape["gx"], mesh.shape["gy"])

    def body(links, incoming):
        dirs, _, _, _, wx, wy, _, lanes = links.shape
        ts = incoming.shape[6]
        rows = wy * ts
        assert wx <= wy
        turned = links.transpose(0, 1, 2, 3, 4, 6, 5, 7)
        flat = turned.reshape(dirs, COMP, wx, ts + 2, wy, lanes)
        flat_in = incoming.reshape(dirs, COMP, *incoming.shape[4:])
        f32 = jnp.float32

        def vm(*shape):
            return pltpu.VMEM((*shape, lanes), f32)

        field = vm(dirs, COMP, wx, rows)
        pairs = vm(dirs, dirs, COMP, wx, rows)
        halo = vm(dirs, COMP, rows)
        scratch = [pltpu.VMEM(flat.shape, f32), pltpu.VMEM(flat_in.shape, f32)]
        scratch += [field, pairs, pairs, pairs, vm(dirs, dirs, COMP, wx + 1, rows), field, field, field]
        scratch += [field, field, vm(dirs, ALG, wx, rows), vm(dirs, dirs, ALG, wx, rows)]
        scratch += [vm(dirs, dirs, ALG, wx + 1, rows), vm(dirs, ALG, wx, rows)]
        scratch += [halo] * 3 + [vm(SENT, wy), vm(SENT, wx), vm(COMP, wy), vm(COMP, wx)]
        scratch += [vm(dirs, SENT, rows)] * 2 + [vm(dirs, ALG, rows)] * 5
        scratch += [pltpu.SemaphoreType.DMA((2,))] + [pltpu.SemaphoreType.DMA((22,))] * 2
        result = pl.pallas_call(
            partial(kernel, sizes),
            out_shape=jax.ShapeDtypeStruct((dirs, COMP, wx, rows, lanes), f32),
            in_specs=[pl.BlockSpec(memory_space=pl.ANY)] * 2,
            out_specs=pl.BlockSpec(memory_space=pltpu.VMEM),
            scratch_shapes=scratch,
            compiler_params=pltpu.CompilerParams(
                collective_id=0, has_side_effects=True, vmem_limit_bytes=60 << 20),
            name="stout",
        )(flat, flat_in)
        return result.reshape(incoming.shape)

    placed = P(None, None, None, None, "gx", "gy", None, None)
    return jax.shard_map(
        body, mesh=mesh, in_specs=(placed, placed), out_specs=placed, check_vma=False)
```
